32 devices in a mesh: parts: 2 (over x), row: 16 (over z, y, core).
Axes of the slice: x: 2, y: 2, z: 4, core: 2. Of those that a mesh axis runs over, the one named last changes fastest.
Arguments:
- tile_values: bfloat16 [2048, 128, 128], P(('parts', 'row')), parts along dimension 0, may hold values from -0.09375 to 0.09375
- tile_row: int32 [2048], P(('parts', 'row')), parts along dimension 0, may hold values from 0 to 1
- tile_col: int32 [2048], P(('parts', 'row')), parts along dimension 0, may hold values from 0 to 15
- primal_start: float32 [4096, 128], P(('parts', 'row')), parts along dimension 0, may hold values from 0 to 1
- objective: float32 [4096, 128], P(('parts', 'row')), parts along dimension 0, may hold values from -3 to 3
- upper_bound: float32 [4096], P(('parts', 'row')), parts along dimension 0, may hold values from 0.3 to 3
- dual_start: float32 [8192, 128], P(('parts', 'row')), parts along dimension 0, may hold values from 0 to 1
- row_bound: float32 [8192, 128], P(('parts', 'row')), parts along dimension 0, may hold values from -6 to 6
Outputs:
- primal: float32 [4096, 128], P(('parts', 'row')), parts along dimension 0
- dual: float32 [8192, 128], P(('parts', 'row')), parts along dimension 0
The draws below stay inside these ranges and needn't reach their ends.
There are 2 independent parts, one for each index of `parts`. The reference program is written for one: setup_inputs(seed, part) draws one part's arguments, and reference() takes and returns one part's arrays. A program takes and returns all parts, laid end to end along the dimension named above; each array names one. Nothing has to cross between parts.
All inputs are finite; a program needn't handle non-finite values.
Results may differ from the reference program's by a relative error of at most 0.0023.
Values may be sent and summed in bfloat16 or wider, within the bound.
A program may use at most 64 MiB of HBM per device.

```python
import math
import jax
import jax.numpy as jnp
from jax import lax

S = 128
TB = 128
TILES_DEV = 64
RB_DEV = 2
ITERS = 3
NTILES = 1024
NRB = 32
NCB = 16
NROWS = 4096
NCOLS = 2048
N_ROW = 16


def plant(array, rng, low, high):
    place = [jax.random.randint(jax.random.fold_in(rng, axis), (), 0, length) for axis, length in enumerate(array.shape)]
    widest = array.shape.index(max(array.shape))
    next_to = place[:widest] + [(place[widest] + 1) % array.shape[widest]] + place[widest + 1:]
    return array.at[tuple(place)].set(low).at[tuple(next_to)].set(high)


def block_levels(stream_key, extent, cuts, low, high):
    def one(axis_at, parts):
        heights = jax.random.uniform(jax.random.fold_in(jax.random.fold_in(stream_key, 6), axis_at), (parts,), jnp.float32, low / len(cuts), high / len(cuts))
        return jnp.repeat(jnp.exp(heights), extent[axis_at] // parts).reshape((-1,) + (1,) * (len(extent) - axis_at - 1))

    gain = one(*cuts[0])
    for cut in cuts[1:]:
        gain = gain * one(*cut)
    return gain


def gaussian(stream_key, dims, width, limit, cuts=(), held_as=jnp.bfloat16):
    drawn = jax.random.normal(stream_key, dims, jnp.float32) * width
    if len(cuts) > 0:
        drawn = block_levels(stream_key, dims, cuts, -0.22, 0.18) * drawn
    return jnp.clip(drawn, min=-limit, max=limit).astype(held_as)


def setup_inputs(seed: int = 0, part: int = 0) -> dict:
    streams_of = jax.random.split(jax.random.key(seed), 9)
    part_keys = jax.random.split(jax.random.fold_in(streams_of[8], part), 9)
    tile_values = gaussian(part_keys[0], (NTILES, TB, TB), (TB * TILES_DEV // RB_DEV) ** -0.5, 0.09375, ((0, 16),))
    tile_row = plant(jax.random.randint(part_keys[1], (NTILES,), 0, RB_DEV), jax.random.fold_in(part_keys[1], 1), 0, RB_DEV - 1).astype(jnp.int32)
    tile_col = plant(jax.random.randint(part_keys[2], (NTILES,), 0, NCB), jax.random.fold_in(part_keys[2], 1), 0, NCB - 1).astype(jnp.int32)
    primal_start = jnp.clip(1.0 * jax.random.uniform(part_keys[3], (NCOLS, S), jnp.float32) ** block_levels(part_keys[3], (NCOLS, S), ((0, 16),), -0.2, 0.2), 0.0, 1.0)
    objective = gaussian(part_keys[4], (NCOLS, S), 0.5, 3.0, ((0, 16),), jnp.float32)
    upper_bound = jnp.clip(jnp.exp(math.log(3.0) - 2.3025851 * jax.random.uniform(part_keys[5], (NCOLS,), jnp.float32) ** block_levels(part_keys[5], (NCOLS,), ((0, 16),), -0.2, 0.2)), 0.3, 3.0)
    dual_start = jnp.clip(1.0 * jax.random.uniform(part_keys[6], (NROWS, S), jnp.float32) ** block_levels(part_keys[6], (NROWS, S), ((0, 16),), -0.2, 0.2), 0.0, 1.0)
    row_bound = gaussian(part_keys[7], (NROWS, S), 1.0, 6.0, ((0, 16),), jnp.float32)
    return {"tile_values": tile_values, "tile_row": tile_row, "tile_col": tile_col, "primal_start": primal_start, "objective": objective, "upper_bound": upper_bound, "dual_start": dual_start, "row_bound": row_bound}


def reference(tile_values, tile_row, tile_col, primal_start, objective, upper_bound, dual_start, row_bound):
    stacked = tile_values.reshape(N_ROW, TILES_DEV, TB, TB)
    rows_local = tile_row.reshape(N_ROW, TILES_DEV).astype(jnp.int32)
    offsets = (jnp.arange(N_ROW, dtype=jnp.int32) * RB_DEV)[:, None]
    rows_global = (rows_local + offsets).astype(jnp.int32)
    cols_here = tile_col.reshape(N_ROW, TILES_DEV).astype(jnp.int32)
    primal = primal_start
    dual = dual_start
    for iteration in range(ITERS):
        dual_blocks = dual.astype(jnp.bfloat16).reshape(NRB, TB, S)

        def add_device(total, inputs):
            values, rows_now, cols_now = inputs
            picked = dual_blocks[rows_now].astype(jnp.float32)
            partial_value = jnp.einsum('tij,tis->tjs', values.astype(jnp.float32), picked)
            return total + jax.ops.segment_sum(partial_value, cols_now, num_segments=NCB), None

        column_sum, _ = lax.scan(add_device, jnp.zeros((NCB, TB, S), jnp.float32), (stacked, rows_global, cols_here))
        column_sum = column_sum.reshape(NCOLS, S)
        updated = jnp.clip(primal - 0.4 * (objective - column_sum), 0.0, upper_bound[:, None])
        extrapolated = (2.0 * updated - primal).astype(jnp.bfloat16).reshape(NCB, TB, S)

        def image_device(carry, inputs):
            values, rows_now, cols_now = inputs
            chosen = extrapolated[cols_now].astype(jnp.float32)
            products = jnp.einsum('tij,tjs->tis', values.astype(jnp.float32), chosen)
            return carry, jax.ops.segment_sum(products, rows_now, num_segments=RB_DEV)

        _, images = lax.scan(image_device, jnp.zeros((), jnp.float32), (stacked, rows_local, cols_here))
        row_image = images.reshape(NROWS, S)
        dual = jnp.maximum(dual + 0.4 * (row_bound - row_image), 0.0)
        primal = updated
    return primal, dual
```

```python
import functools

import jax
import jax.numpy as jnp
from jax import lax
from jax.experimental import pallas as pl
from jax.experimental.pallas import tpu as pltpu
from jax.sharding import PartitionSpec as P

ITERS = 3
STEP = 0.4
F32 = jnp.float32
BF16 = jnp.bfloat16


def dense_kernel(group, row_blocks, rows, cols, tiles, high, low, total):
    step = pl.program_id(0)

    @pl.when(step == 0)
    def _():
        total[...] = jnp.zeros_like(total)

    for i in range(group):
        t = step * group + i
        at = cols[t] * row_blocks + rows[t]
        total[at] += tiles[i].astype(F32)

    @pl.when(step == pl.num_programs(0) - 1)
    def _():
        @pl.loop(0, total.shape[0])
        def _(b):
            value = total[b]
            rounded = value.astype(BF16)
            high[b] = rounded
            low[b] = (value - rounded.astype(F32)).astype(BF16)


def dense(tile_values, tile_row, tile_col, blocks, row_blocks):
    tiles, size, _ = tile_values.shape
    group = 8
    whole = pl.BlockSpec((blocks * row_blocks, size, size), lambda i, r, c: (0, 0, 0))
    shape = jax.ShapeDtypeStruct((blocks * row_blocks, size, size), BF16)
    return pl.pallas_call(
        functools.partial(dense_kernel, group, row_blocks),
        out_shape=(shape, shape),
        grid_spec=pltpu.PrefetchScalarGridSpec(
            num_scalar_prefetch=2,
            grid=(tiles // group,),
            in_specs=[pl.BlockSpec((group, size, size), lambda i, r, c: (i, 0, 0))],
            out_specs=(whole, whole),
            scratch_shapes=[pltpu.VMEM((blocks * row_blocks, size, size), F32)],
        ),
        compiler_params=pltpu.CompilerParams(dimension_semantics=("arbitrary",)),
    )(tile_row, tile_col, tile_values)


def iterate_kernel(
    n, high, low, primal_start, objective, upper, dual_start, row_bound,
    primal, dual,
    bound, own, send1, recv1, send2, recv2, same, other,
    s1, r1, s2, r2, sx, rx, sf, rf,
):
    me = lax.axis_index("row")
    core = lax.rem(me, 2)
    chip = me // 2
    chips = n // 2
    partner = me + 1 - 2 * core

    def peer(d):
        return lax.rem(chip + d, chips) * 2 + core

    def send(src, dst, send_sem, recv_sem, device):
        return pltpu.make_async_remote_copy(
            src_ref=src, dst_ref=dst, send_sem=send_sem, recv_sem=recv_sem,
            device_id={"row": device}, device_id_type=pl.DeviceIdType.MESH,
        )

    def to_partner(d):
        return send(send1.at[d], recv1.at[d], s1.at[d], r1.at[d], partner)

    def to_peer(d):
        return send(send2.at[d], recv2.at[d], s2.at[d], r2.at[d], peer(d))

    def spread(d):
        return send(same.at[0], same.at[d], sx.at[d], rx.at[d], peer(d))

    def forward(d):
        return send(same.at[d], other.at[d], sf.at[d], rf.at[d], partner)

    barrier = pltpu.get_barrier_semaphore()
    pl.semaphore_signal(
        barrier, inc=1, device_id={"row": partner}, device_id_type=pl.DeviceIdType.MESH
    )
    for d in range(1, chips):
        pl.semaphore_signal(
            barrier, inc=1, device_id={"row": peer(d)}, device_id_type=pl.DeviceIdType.MESH
        )
    size = primal.shape[0]
    primal[...] = primal_start[...]
    dual[...] = dual_start[...]
    bound[...] = jnp.broadcast_to(upper[...], (size, size)).T
    pl.semaphore_wait(barrier, chips)

    order = list(range(1, chips)) + [0]

    def iteration(_, carry):
        lowered = dual[...].T.astype(BF16)
        for d in order:
            k = lax.rem(chip + d, chips)
            mine, theirs = 2 * k + core, 2 * k + 1 - core
            pair = jnp.dot(
                lowered, jnp.concatenate([high[theirs], high[mine]], axis=1),
                preferred_element_type=F32,
            ) + jnp.dot(
                lowered, jnp.concatenate([low[theirs], low[mine]], axis=1),
                preferred_element_type=F32,
            )
            send1[d] = pair[:, :size].astype(BF16)
            to_partner(d).start()
            own[d] = pair[:, size:]
        for d in range(1, chips):
            to_partner(d).wait_recv()
            send2[d] = (own[d] + recv1[d].astype(F32)).astype(BF16)
            to_peer(d).start()
        to_partner(0).wait_recv()
        total = own[0] + recv1[0].astype(F32)
        for d in range(1, chips):
            to_peer(d).wait_recv()
            total += recv2[d].astype(F32)
        before = primal[...]
        updated = jnp.clip(before - STEP * (objective[...] - total.T), 0.0, bound[...])
        same[0] = (2.0 * updated - before).astype(BF16)
        for d in range(1, chips):
            spread(d).start()
        forward(0).start()
        primal[...] = updated

        def product(c, block):
            return jnp.dot(high[c], block, preferred_element_type=F32) + jnp.dot(
                low[c], block, preferred_element_type=F32
            )

        image = product(2 * chip + core, same[0])
        for d in range(1, chips):
            spread(d).wait_recv()
            forward(d).start()
            image += product(2 * lax.rem(chip + chips - d, chips) + core, same[d])
        for d in range(chips):
            forward(d).wait_recv()
            image += product(2 * lax.rem(chip + chips - d, chips) + 1 - core, other[d])
        dual[...] = jnp.maximum(dual[...] + STEP * (row_bound[...] - image), 0.0)
        for d in range(chips):
            to_partner(d).wait_send()
            forward(d).wait_send()
            if d:
                to_peer(d).wait_send()
                spread(d).wait_send()
        return carry

    lax.fori_loop(0, ITERS, iteration, 0)


def body(
    tile_values, tile_row, tile_col, primal_start, objective, upper_bound, dual_start, row_bound
):
    n = lax.axis_size("row")
    size = tile_values.shape[1]
    blocks = n * primal_start.shape[0] // size
    assert blocks == n and primal_start.shape[1] == size and n % 2 == 0
    row_blocks = dual_start.shape[0] // size
    high, low = dense(tile_values, tile_row, tile_col, blocks, row_blocks)
    chips = n // 2
    vmem = pl.BlockSpec(memory_space=pltpu.VMEM)
    half = pltpu.VMEM((chips, size, size), BF16)
    return pl.pallas_call(
        functools.partial(iterate_kernel, n),
        out_shape=(
            jax.ShapeDtypeStruct(primal_start.shape, F32),
            jax.ShapeDtypeStruct(dual_start.shape, F32),
        ),
        in_specs=[vmem] * 7,
        out_specs=(vmem, vmem),
        scratch_shapes=[
            pltpu.VMEM((size, size), F32),
            pltpu.VMEM((chips, size, size), F32),
            half, half, half, half, half, half,
        ] + [pltpu.SemaphoreType.DMA((chips,))] * 8,
        compiler_params=pltpu.CompilerParams(
            collective_id=0, has_side_effects=True, vmem_limit_bytes=60000 * 1024
        ),
    )(
        high.reshape(blocks, row_blocks * size, size),
        low.reshape(blocks, row_blocks * size, size),
        primal_start, objective, upper_bound.reshape(1, -1), dual_start, row_bound,
    )


def solution(mesh):
    rows = P(("parts", "row"), None)
    flat = P(("parts", "row"))
    return jax.shard_map(
        body,
        mesh=mesh,
        in_specs=(P(("parts", "row"), None, None), flat, flat, rows, rows, flat, rows, rows),
        out_specs=(rows, rows),
        check_vma=False,
    )
```

```python
import functools

import jax
import jax.numpy as jnp
from jax import lax
from jax.experimental import pallas as pl
from jax.experimental.pallas import tpu as pltpu
from jax.sharding import PartitionSpec as P

ITERS = 3
HALVES = 2
STEP = 0.4
F32 = jnp.float32
BF16 = jnp.bfloat16


def dense_kernel(chunks, row_blocks, rows, cols, tiles, high, low, total, held, arrived):
    group = held.shape[0] // chunks

    def copy(k):
        part = pl.ds(k * group, group)
        return pltpu.make_async_copy(tiles.at[part], held.at[part], arrived.at[k])

    for k in range(chunks):
        copy(k).start()
    total[...] = jnp.zeros_like(total)
    for k in range(chunks):
        copy(k).wait()

        @pl.loop(0, group, unroll=min(group, 8))
        def _(i):
            t = k * group + i
            at = cols[t] * row_blocks + rows[t]
            total[at] += held[t].astype(F32)

    @pl.loop(0, total.shape[0], unroll=4)
    def _(b):
        value = total[b]
        rounded = value.astype(BF16)
        high[b] = rounded
        low[b] = (value - rounded.astype(F32)).astype(BF16)


def dense(tile_values, tile_row, tile_col, blocks, row_blocks):
    tiles, size, _ = tile_values.shape
    chunks = 8
    shape = jax.ShapeDtypeStruct((blocks * row_blocks, size, size), BF16)
    smem = pl.BlockSpec(memory_space=pltpu.SMEM)
    vmem = pl.BlockSpec(memory_space=pltpu.VMEM)
    room = size * size * (4 * blocks * row_blocks + 2 * tiles + 4 * blocks * row_blocks)
    return pl.pallas_call(
        functools.partial(dense_kernel, chunks, row_blocks),
        out_shape=(shape, shape),
        in_specs=[smem, smem, pl.BlockSpec(memory_space=pltpu.HBM)],
        out_specs=(vmem, vmem),
        scratch_shapes=[
            pltpu.VMEM((blocks * row_blocks, size, size), F32),
            pltpu.VMEM((tiles, size, size), BF16),
            pltpu.SemaphoreType.DMA((chunks,)),
        ],
        compiler_params=pltpu.CompilerParams(vmem_limit_bytes=room + (4 << 20)),
    )(tile_row, tile_col, tile_values)


def iterate_kernel(
    n, halves, high, low, primal_start, objective, upper, dual_start, row_bound,
    primal_out, dual_out,
    primal, dual, cost, bound, own, send1, recv1, send2, recv2, same, other,
    s1, r1, s2, r2, sx, rx, sf, rf,
):
    me = lax.axis_index("row")
    core = lax.rem(me, 2)
    chip = me // 2
    chips = n // 2
    partner = me + 1 - 2 * core
    size = primal.shape[1]
    part = primal.shape[0] // halves

    def peer(d):
        return lax.rem(chip + d, chips) * 2 + core

    def source(d):
        return lax.rem(chip + chips - d, chips) * 2

    def send(src, dst, send_sem, recv_sem, device):
        return pltpu.make_async_remote_copy(
            src_ref=src, dst_ref=dst, send_sem=send_sem, recv_sem=recv_sem,
            device_id={"row": device}, device_id_type=pl.DeviceIdType.MESH,
        )

    def to_partner(h, d):
        return send(send1.at[h, d], recv1.at[h, d], s1.at[h, d], r1.at[h, d], partner)

    def to_peer(h, d):
        return send(send2.at[h, d], recv2.at[h, d], s2.at[h, d], r2.at[h, d], peer(d))

    def spread(h, d):
        return send(same.at[h, 0], same.at[h, d], sx.at[h, d], rx.at[h, d], peer(d))

    def forward(h, d):
        return send(same.at[h, d], other.at[h, d], sf.at[h, d], rf.at[h, d], partner)

    order = list(range(1, chips)) + [0]

    def scenarios(h):
        return pl.ds(h * part, part)

    def partials(h, start):
        lowered = dual[scenarios(h), :].astype(BF16)
        for d in order:
            k = lax.rem(chip + d, chips)
            mine, theirs = 2 * k + core, 2 * k + 1 - core
            pair = jnp.dot(
                lowered, jnp.concatenate([high[theirs], high[mine]], axis=1),
                preferred_element_type=F32,
            ) + jnp.dot(
                lowered, jnp.concatenate([low[theirs], low[mine]], axis=1),
                preferred_element_type=F32,
            )
            send1[h, d] = pair[:, :size].astype(BF16)
            if start:
                to_partner(h, d).start()
            own[h, d] = pair[:, size:]

    def add_partner(h):
        for d in range(1, chips):
            to_partner(h, d).wait_recv()
            send2[h, d] = (own[h, d] + recv1[h, d].astype(F32)).astype(BF16)
            to_peer(h, d).start()

    def update(h):
        to_partner(h, 0).wait_recv()
        total = own[h, 0] + recv1[h, 0].astype(F32)
        for d in range(1, chips):
            to_peer(h, d).wait_recv()
            total += recv2[h, d].astype(F32)
        before = primal[scenarios(h), :]
        updated = jnp.clip(before - STEP * (cost[scenarios(h), :] - total), 0.0, upper[...])
        same[h, 0] = (2.0 * updated - before).astype(BF16)
        for d in range(1, chips):
            spread(h, d).start()
        forward(h, 0).start()
        primal[scenarios(h), :] = updated
        for d in range(chips):
            to_partner(h, d).wait_send()

    def pass_on(h):
        for d in range(1, chips):
            spread(h, d).wait_recv()
            forward(h, d).start()
        for d in range(1, chips):
            to_peer(h, d).wait_send()

    def image(h):
        total = jnp.zeros((part, dual.shape[1]), F32)
        for d in range(chips):
            forward(h, d).wait_recv()
            block = jnp.concatenate([same[h, d], other[h, d]], axis=1)
            a, b = source(d) + core, source(d) + 1 - core
            for ref in (high, low):
                total += lax.dot_general(
                    block, jnp.concatenate([ref[a], ref[b]], axis=1),
                    (((1,), (1,)), ((), ())), preferred_element_type=F32,
                )
        dual[scenarios(h), :] = jnp.maximum(
            dual[scenarios(h), :] + STEP * (bound[scenarios(h), :] - total), 0.0
        )
        for d in range(chips):
            forward(h, d).wait_send()
            if d:
                spread(h, d).wait_send()

    barrier = pltpu.get_barrier_semaphore()
    pl.semaphore_signal(
        barrier, inc=1, device_id={"row": partner}, device_id_type=pl.DeviceIdType.MESH
    )
    for d in range(1, chips):
        pl.semaphore_signal(
            barrier, inc=1, device_id={"row": peer(d)}, device_id_type=pl.DeviceIdType.MESH
        )
    dual[...] = dual_start[...].T
    for h in range(halves):
        partials(h, False)
    primal[...] = primal_start[...].T
    cost[...] = objective[...].T
    bound[...] = row_bound[...].T
    pl.semaphore_wait(barrier, chips)
    for h in range(halves):
        for d in order:
            to_partner(h, d).start()
    for h in range(halves):
        add_partner(h)

    def iteration(step, carry):
        more = step < ITERS - 1
        for h in range(halves):
            update(h)
        for h in range(halves):
            pass_on(h)
            if h:
                pl.when(more)(functools.partial(add_partner, h - 1))
            image(h)
            pl.when(more)(functools.partial(partials, h, True))
        pl.when(more)(functools.partial(add_partner, halves - 1))
        return carry

    lax.fori_loop(0, ITERS, iteration, 0)
    primal_out[...] = primal[...].T
    dual_out[...] = dual[...].T


def body(
    tile_values, tile_row, tile_col, primal_start, objective, upper_bound, dual_start, row_bound
):
    n = lax.axis_size("row")
    size = tile_values.shape[1]
    count = primal_start.shape[1]
    blocks = n * primal_start.shape[0] // size
    assert blocks == n and n % 2 == 0
    rows = dual_start.shape[0]
    row_blocks = rows // size
    high, low = dense(tile_values, tile_row, tile_col, blocks, row_blocks)
    chips = n // 2
    halves = HALVES
    part = count // halves
    vmem = pl.BlockSpec(memory_space=pltpu.VMEM)
    buffer = pltpu.VMEM((halves, chips, part, size), BF16)
    state = pltpu.VMEM((count, size), F32)
    long_state = pltpu.VMEM((count, rows), F32)
    room = 4 * blocks * rows * size + 16 * chips * count * size + (6 << 20)
    return pl.pallas_call(
        functools.partial(iterate_kernel, n, halves),
        out_shape=(
            jax.ShapeDtypeStruct(primal_start.shape, F32),
            jax.ShapeDtypeStruct(dual_start.shape, F32),
        ),
        in_specs=[vmem] * 7,
        out_specs=(vmem, vmem),
        scratch_shapes=[
            state, long_state, state, long_state,
            pltpu.VMEM((halves, chips, part, size), F32),
            buffer, buffer, buffer, buffer, buffer, buffer,
        ] + [pltpu.SemaphoreType.DMA((halves, chips))] * 8,
        compiler_params=pltpu.CompilerParams(
            collective_id=0, has_side_effects=True, vmem_limit_bytes=room
        ),
    )(
        high.reshape(blocks, rows, size), low.reshape(blocks, rows, size),
        primal_start, objective, upper_bound.reshape(1, -1), dual_start, row_bound,
    )


def solution(mesh):
    rows = P(("parts", "row"), None)
    flat = P(("parts", "row"))
    return jax.shard_map(
        body,
        mesh=mesh,
        in_specs=(P(("parts", "row"), None, None), flat, flat, rows, rows, flat, rows, rows),
        out_specs=(rows, rows),
        check_vma=False,
    )
```

```python
import functools

import jax
import jax.numpy as jnp
from jax import lax
from jax.experimental import pallas as pl
from jax.experimental.pallas import tpu as pltpu
from jax.sharding import PartitionSpec as P

ITERS = 3
HALVES = 2
STEP = 0.4
F32 = jnp.float32
BF16 = jnp.bfloat16


def dense_kernel(chunks, row_blocks, rows, cols, tiles, high, low, total, held, arrived):
    group = held.shape[0] // chunks

    def copy(k):
        part = pl.ds(k * group, group)
        return pltpu.make_async_copy(tiles.at[part], held.at[part], arrived.at[k])

    for k in range(chunks):
        copy(k).start()
    total[...] = jnp.zeros_like(total)
    for k in range(chunks):
        copy(k).wait()

        @pl.loop(0, group, unroll=min(group, 8))
        def _(i):
            t = k * group + i
            at = cols[t] * row_blocks + rows[t]
            total[at] += held[t].astype(F32)

    @pl.loop(0, total.shape[0], unroll=4)
    def _(b):
        value = total[b]
        rounded = value.astype(BF16)
        high[b] = rounded
        low[b] = (value - rounded.astype(F32)).astype(BF16)


def dense(tile_values, tile_row, tile_col, blocks, row_blocks):
    tiles, size, _ = tile_values.shape
    chunks = 8
    shape = jax.ShapeDtypeStruct((blocks * row_blocks, size, size), BF16)
    smem = pl.BlockSpec(memory_space=pltpu.SMEM)
    vmem = pl.BlockSpec(memory_space=pltpu.VMEM)
    room = size * size * (4 * blocks * row_blocks + 2 * tiles + 4 * blocks * row_blocks)
    return pl.pallas_call(
        functools.partial(dense_kernel, chunks, row_blocks),
        out_shape=(shape, shape),
        in_specs=[smem, smem, pl.BlockSpec(memory_space=pltpu.HBM)],
        out_specs=(vmem, vmem),
        scratch_shapes=[
            pltpu.VMEM((blocks * row_blocks, size, size), F32),
            pltpu.VMEM((tiles, size, size), BF16),
            pltpu.SemaphoreType.DMA((chunks,)),
        ],
        compiler_params=pltpu.CompilerParams(vmem_limit_bytes=room + (4 << 20)),
    )(tile_row, tile_col, tile_values)


def iterate_kernel(
    n, halves, high, low, primal_start, objective, upper, dual_start, row_bound,
    primal_out, dual_out,
    primal, dual, cost, bound, own, send1, recv1, send2, recv2, same, other,
    s1, r1, s2, r2, sx, rx, sf, rf,
):
    me = lax.axis_index("row")
    core = lax.rem(me, 2)
    chip = me // 2
    chips = n // 2
    partner = me + 1 - 2 * core
    size = primal.shape[1]
    part = primal.shape[0] // halves

    def peer(d):
        return lax.rem(chip + d, chips) * 2 + core

    def source(d):
        return lax.rem(chip + chips - d, chips) * 2

    def send(src, dst, send_sem, recv_sem, device):
        return pltpu.make_async_remote_copy(
            src_ref=src, dst_ref=dst, send_sem=send_sem, recv_sem=recv_sem,
            device_id={"row": device}, device_id_type=pl.DeviceIdType.MESH,
        )

    def to_partner(h, d):
        return send(send1.at[h, d], recv1.at[h, d], s1.at[h, d], r1.at[h, d], partner)

    def to_peer(h, d):
        return send(send2.at[h, d], recv2.at[h, d], s2.at[h, d], r2.at[h, d], peer(d))

    def spread(h, d):
        return send(same.at[h, 0], same.at[h, d], sx.at[h, d], rx.at[h, d], peer(d))

    def forward(h, d):
        return send(same.at[h, d], other.at[h, d], sf.at[h, d], rf.at[h, d], partner)

    order = list(range(1, chips)) + [0]

    def scenarios(h):
        return pl.ds(h * part, part)

    def wide(left, blocks, axis):
        total = None
        for ref in (high, low):
            right = jnp.concatenate([ref[c] for c in blocks], axis=1)
            value = lax.dot_general(
                left, right, (((1,), (axis,)), ((), ())), preferred_element_type=F32
            )
            total = value if total is None else total + value
        return total

    def partials(h, start):
        lowered = dual[scenarios(h), :].astype(BF16)
        for own_side in (False, True):
            for i in range(0, chips, 2):
                pair = order[i : i + 2]
                side = core if own_side else 1 - core
                value = wide(lowered, [lax.rem(chip + d, chips) * 2 + side for d in pair], 0)
                for j, d in enumerate(pair):
                    piece = value[:, j * size : (j + 1) * size]
                    if own_side:
                        own[h, d] = piece
                    else:
                        send1[h, d] = piece.astype(BF16)
                        if start:
                            to_partner(h, d).start()

    def add_partner(h):
        for d in range(1, chips):
            to_partner(h, d).wait_recv()
            send2[h, d] = (own[h, d] + recv1[h, d].astype(F32)).astype(BF16)
            to_peer(h, d).start()

    def update(h):
        to_partner(h, 0).wait_recv()
        total = own[h, 0] + recv1[h, 0].astype(F32)
        for d in range(1, chips):
            to_peer(h, d).wait_recv()
            total += recv2[h, d].astype(F32)
        before = primal[scenarios(h), :]
        updated = jnp.clip(before - STEP * (cost[scenarios(h), :] - total), 0.0, upper[...])
        same[h, 0] = (2.0 * updated - before).astype(BF16)
        for d in range(1, chips):
            spread(h, d).start()
        forward(h, 0).start()
        primal[scenarios(h), :] = updated
        for d in range(chips):
            to_partner(h, d).wait_send()

    def pass_on(h):
        for d in range(1, chips):
            spread(h, d).wait_recv()
            forward(h, d).start()
        for d in range(1, chips):
            to_peer(h, d).wait_send()

    def image(h):
        total = None
        for held, side in ((same, core), (other, 1 - core)):
            for i in range(0, chips, 2):
                pair = (i, i + 1)
                if held is other:
                    for d in pair:
                        forward(h, d).wait_recv()
                block = jnp.concatenate([held[h, d] for d in pair], axis=1)
                value = wide(block, [source(d) + side for d in pair], 1)
                total = value if total is None else total + value
        dual[scenarios(h), :] = jnp.maximum(
            dual[scenarios(h), :] + STEP * (bound[scenarios(h), :] - total), 0.0
        )
        for d in range(chips):
            forward(h, d).wait_send()
            if d:
                spread(h, d).wait_send()

    barrier = pltpu.get_barrier_semaphore()
    pl.semaphore_signal(
        barrier, inc=1, device_id={"row": partner}, device_id_type=pl.DeviceIdType.MESH
    )
    for d in range(1, chips):
        pl.semaphore_signal(
            barrier, inc=1, device_id={"row": peer(d)}, device_id_type=pl.DeviceIdType.MESH
        )
    dual[...] = dual_start[...].T
    for h in range(halves):
        partials(h, False)
    primal[...] = primal_start[...].T
    cost[...] = objective[...].T
    bound[...] = row_bound[...].T
    pl.semaphore_wait(barrier, chips)
    for h in range(halves):
        for d in order:
            to_partner(h, d).start()
    for h in range(halves):
        add_partner(h)

    def iteration(step, carry):
        more = step < ITERS - 1
        for h in range(halves):
            update(h)
        for h in range(halves):
            pass_on(h)
            if h:
                pl.when(more)(functools.partial(add_partner, h - 1))
            image(h)
            pl.when(more)(functools.partial(partials, h, True))
        pl.when(more)(functools.partial(add_partner, halves - 1))
        return carry

    lax.fori_loop(0, ITERS, iteration, 0)
    primal_out[...] = primal[...].T
    dual_out[...] = dual[...].T


def body(
    tile_values, tile_row, tile_col, primal_start, objective, upper_bound, dual_start, row_bound
):
    n = lax.axis_size("row")
    size = tile_values.shape[1]
    count = primal_start.shape[1]
    blocks = n * primal_start.shape[0] // size
    assert blocks == n and n % 4 == 0
    rows = dual_start.shape[0]
    row_blocks = rows // size
    high, low = dense(tile_values, tile_row, tile_col, blocks, row_blocks)
    chips = n // 2
    halves = HALVES
    part = count // halves
    vmem = pl.BlockSpec(memory_space=pltpu.VMEM)
    buffer = pltpu.VMEM((halves, chips, part, size), BF16)
    state = pltpu.VMEM((count, size), F32)
    long_state = pltpu.VMEM((count, rows), F32)
    room = 4 * blocks * rows * size + 16 * chips * count * size + (6 << 20)
    return pl.pallas_call(
        functools.partial(iterate_kernel, n, halves),
        out_shape=(
            jax.ShapeDtypeStruct(primal_start.shape, F32),
            jax.ShapeDtypeStruct(dual_start.shape, F32),
        ),
        in_specs=[vmem] * 7,
        out_specs=(vmem, vmem),
        scratch_shapes=[
            state, long_state, state, long_state,
            pltpu.VMEM((halves, chips, part, size), F32),
            buffer, buffer, buffer, buffer, buffer, buffer,
        ] + [pltpu.SemaphoreType.DMA((halves, chips))] * 8,
        compiler_params=pltpu.CompilerParams(
            collective_id=0, has_side_effects=True, vmem_limit_bytes=room
        ),
    )(
        high.reshape(blocks, rows, size), low.reshape(blocks, rows, size),
        primal_start, objective, upper_bound.reshape(1, -1), dual_start, row_bound,
    )


def solution(mesh):
    rows = P(("parts", "row"), None)
    flat = P(("parts", "row"))
    return jax.shard_map(
        body,
        mesh=mesh,
        in_specs=(P(("parts", "row"), None, None), flat, flat, rows, rows, flat, rows, rows),
        out_specs=(rows, rows),
        check_vma=False,
    )
```

```python
import functools

import jax
import jax.numpy as jnp
from jax import lax
from jax.experimental import pallas as pl
from jax.experimental.pallas import tpu as pltpu
from jax.sharding import PartitionSpec as P

ITERS = 3
HALVES = 2
STEP = 0.4
F32 = jnp.float32
BF16 = jnp.bfloat16


def dense_kernel(places, tiles, high, low, total):
    total[...] = jnp.zeros_like(total)

    @pl.loop(0, tiles.shape[0], unroll=8)
    def _(t):
        total[places[t]] += tiles[t].astype(F32)

    @pl.loop(0, total.shape[0], unroll=4)
    def _(b):
        value = total[b]
        rounded = value.astype(BF16)
        high[b] = rounded
        low[b] = (value - rounded.astype(F32)).astype(BF16)


def dense(tile_values, tile_row, tile_col, blocks, row_blocks):
    tiles, size, _ = tile_values.shape
    shape = jax.ShapeDtypeStruct((blocks * row_blocks, size, size), BF16)
    smem = pl.BlockSpec(memory_space=pltpu.SMEM)
    vmem = pl.BlockSpec(memory_space=pltpu.VMEM)
    room = size * size * (8 * blocks * row_blocks + 2 * tiles)
    return pl.pallas_call(
        dense_kernel,
        out_shape=(shape, shape),
        in_specs=[smem, vmem],
        out_specs=(vmem, vmem),
        scratch_shapes=[pltpu.VMEM((blocks * row_blocks, size, size), F32)],
        compiler_params=pltpu.CompilerParams(vmem_limit_bytes=room + (4 << 20)),
    )(tile_col * row_blocks + tile_row, tile_values)


def iterate_kernel(
    n, halves, high, low, primal_start, objective, upper, dual_start, row_bound,
    primal_out, dual_out,
    primal, dual, cost, bound, own, send1, recv1, send2, recv2, same, other,
    s1, r1, s2, r2, sx, rx, sf, rf,
):
    me = lax.axis_index("row")
    core = lax.rem(me, 2)
    chip = me // 2
    chips = n // 2
    partner = me + 1 - 2 * core
    size = primal.shape[1]
    part = primal.shape[0] // halves

    def peer(d):
        return lax.rem(chip + d, chips) * 2 + core

    def source(d):
        return lax.rem(chip + chips - d, chips) * 2

    def send(src, dst, send_sem, recv_sem, device):
        return pltpu.make_async_remote_copy(
            src_ref=src, dst_ref=dst, send_sem=send_sem, recv_sem=recv_sem,
            device_id={"row": device}, device_id_type=pl.DeviceIdType.MESH,
        )

    def to_partner(h, d):
        return send(send1.at[h, d], recv1.at[h, d], s1.at[h, d], r1.at[h, d], partner)

    def to_peer(h, d):
        return send(send2.at[h, d], recv2.at[h, d], s2.at[h, d], r2.at[h, d], peer(d))

    def spread(h, d):
        return send(same.at[h, 0], same.at[h, d], sx.at[h, d], rx.at[h, d], peer(d))

    def forward(h, d):
        return send(same.at[h, d], other.at[h, d], sf.at[h, d], rf.at[h, d], partner)

    order = list(range(1, chips)) + [0]

    def scenarios(h):
        return pl.ds(h * part, part)

    def wide(left, blocks, axis):
        total = None
        for ref in (high, low):
            right = jnp.concatenate([ref[c] for c in blocks], axis=1)
            value = lax.dot_general(
                left, right, (((1,), (axis,)), ((), ())), preferred_element_type=F32
            )
            total = value if total is None else total + value
        return total

    def partials(h, start):
        lowered = dual[scenarios(h), :].astype(BF16)
        for own_side in (False, True):
            for i in range(0, chips, 2):
                pair = order[i : i + 2]
                side = core if own_side else 1 - core
                value = wide(lowered, [lax.rem(chip + d, chips) * 2 + side for d in pair], 0)
                for j, d in enumerate(pair):
                    piece = value[:, j * size : (j + 1) * size]
                    if own_side:
                        own[h, d] = piece
                    else:
                        send1[h, d] = piece.astype(BF16)
                        if start:
                            to_partner(h, d).start()

    def add_partner(h):
        for d in range(1, chips):
            to_partner(h, d).wait_recv()
            send2[h, d] = (own[h, d] + recv1[h, d].astype(F32)).astype(BF16)
            to_peer(h, d).start()

    def update(h):
        to_partner(h, 0).wait_recv()
        total = own[h, 0] + recv1[h, 0].astype(F32)
        for d in range(1, chips):
            to_peer(h, d).wait_recv()
            total += recv2[h, d].astype(F32)
        before = primal[scenarios(h), :]
        updated = jnp.clip(before - STEP * (cost[scenarios(h), :] - total), 0.0, upper[...])
        same[h, 0] = (2.0 * updated - before).astype(BF16)
        for d in range(1, chips):
            spread(h, d).start()
        forward(h, 0).start()
        primal[scenarios(h), :] = updated
        for d in range(chips):
            to_partner(h, d).wait_send()

    def pass_on(h):
        for d in range(1, chips):
            spread(h, d).wait_recv()
            forward(h, d).start()
        for d in range(1, chips):
            to_peer(h, d).wait_send()

    def image(h):
        total = None
        for held, side in ((same, core), (other, 1 - core)):
            for i in range(0, chips, 2):
                pair = (i, i + 1)
                if held is other:
                    for d in pair:
                        forward(h, d).wait_recv()
                block = jnp.concatenate([held[h, d] for d in pair], axis=1)
                value = wide(block, [source(d) + side for d in pair], 1)
                total = value if total is None else total + value
        dual[scenarios(h), :] = jnp.maximum(
            dual[scenarios(h), :] + STEP * (bound[scenarios(h), :] - total), 0.0
        )
        for d in range(chips):
            forward(h, d).wait_send()
            if d:
                spread(h, d).wait_send()

    barrier = pltpu.get_barrier_semaphore()
    pl.semaphore_signal(
        barrier, inc=1, device_id={"row": partner}, device_id_type=pl.DeviceIdType.MESH
    )
    for d in range(1, chips):
        pl.semaphore_signal(
            barrier, inc=1, device_id={"row": peer(d)}, device_id_type=pl.DeviceIdType.MESH
        )
    dual[...] = dual_start[...].T
    for h in range(halves):
        partials(h, False)
    primal[...] = primal_start[...].T
    cost[...] = objective[...].T
    bound[...] = row_bound[...].T
    pl.semaphore_wait(barrier, chips)
    for h in range(halves):
        for d in order:
            to_partner(h, d).start()
    for h in range(halves):
        add_partner(h)

    def iteration(step, carry):
        more = step < ITERS - 1
        for h in range(halves):
            update(h)
        for h in range(halves):
            pass_on(h)
            if h:
                pl.when(more)(functools.partial(add_partner, h - 1))
            image(h)
            pl.when(more)(functools.partial(partials, h, True))
        pl.when(more)(functools.partial(add_partner, halves - 1))
        return carry

    lax.fori_loop(0, ITERS, iteration, 0)
    primal_out[...] = primal[...].T
    dual_out[...] = dual[...].T


def body(
    tile_values, tile_row, tile_col, primal_start, objective, upper_bound, dual_start, row_bound
):
    n = lax.axis_size("row")
    size = tile_values.shape[1]
    count = primal_start.shape[1]
    blocks = n * primal_start.shape[0] // size
    assert blocks == n and n % 4 == 0
    rows = dual_start.shape[0]
    row_blocks = rows // size
    high, low = dense(tile_values, tile_row, tile_col, blocks, row_blocks)
    chips = n // 2
    halves = HALVES
    part = count // halves
    vmem = pl.BlockSpec(memory_space=pltpu.VMEM)
    buffer = pltpu.VMEM((halves, chips, part, size), BF16)
    state = pltpu.VMEM((count, size), F32)
    long_state = pltpu.VMEM((count, rows), F32)
    room = 4 * blocks * rows * size + 16 * chips * count * size + (6 << 20)
    return pl.pallas_call(
        functools.partial(iterate_kernel, n, halves),
        out_shape=(
            jax.ShapeDtypeStruct(primal_start.shape, F32),
            jax.ShapeDtypeStruct(dual_start.shape, F32),
        ),
        in_specs=[vmem] * 7,
        out_specs=(vmem, vmem),
        scratch_shapes=[
            state, long_state, state, long_state,
            pltpu.VMEM((halves, chips, part, size), F32),
            buffer, buffer, buffer, buffer, buffer, buffer,
        ] + [pltpu.SemaphoreType.DMA((halves, chips))] * 8,
        compiler_params=pltpu.CompilerParams(
            collective_id=0, has_side_effects=True, vmem_limit_bytes=room
        ),
    )(
        high.reshape(blocks, rows, size), low.reshape(blocks, rows, size),
        primal_start, objective, upper_bound.reshape(1, -1), dual_start, row_bound,
    )


def solution(mesh):
    rows = P(("parts", "row"), None)
    flat = P(("parts", "row"))
    return jax.shard_map(
        body,
        mesh=mesh,
        in_specs=(P(("parts", "row"), None, None), flat, flat, rows, rows, flat, rows, rows),
        out_specs=(rows, rows),
        check_vma=False,
    )
```
